32 devices in a mesh: groups: 2 (over y), row: 4 (over z), col: 4 (over x, core).
Axes of the slice: x: 2, y: 2, z: 4, core: 2. Of those that a mesh axis runs over, the one named last changes fastest.
Arguments:
- left_act: float32 [256, 32, 32], P(('groups', 'row'), 'col'), parts along dimension 0, may hold values from -6 to 6
- right_act: float32 [256, 32, 32], P(('groups', 'row'), 'col'), parts along dimension 0, may hold values from -6 to 6
- weight: float32 [1024, 128], replicated, may hold values from -0.75 to 0.75
- bias: float32 [128], replicated, may hold values from -1.8 to 1.8
- cotangent: float32 [64, 32, 128], P(('groups', 'row'), 'col'), parts along dimension 0, may hold values from -0.6 to 0.6
Outputs:
- pair: float32 [64, 32, 128], P(('groups', 'row'), 'col'), parts along dimension 0
- grad_left: float32 [256, 32, 32], P(('groups', 'row'), 'col'), parts along dimension 0
- grad_right: float32 [256, 32, 32], P(('groups', 'row'), 'col'), parts along dimension 0
- grad_weight: float32 [2048, 128], P(('groups', 'row')), parts along dimension 0
The draws below stay inside these ranges and needn't reach their ends.
There are 2 independent parts, one for each index of `groups`. The reference program is written for one: setup_inputs(seed, part) draws one part's arguments, and reference() takes and returns one part's arrays. A program takes and returns all parts, laid end to end along the dimension named above; an argument that names none is the same for every part. Nothing has to cross between parts.
All inputs are finite; a program needn't handle non-finite values.
Results may differ from the reference program's by a relative error of at most 0.0003.
Values sent between devices are 32-bit elements; how exact they have to be, the bound alone decides.
A program may use at most 64 MiB of HBM per device.

```python
import math
import jax
import jax.numpy as jnp
from jax import lax

C = 32
Z = 128
S = 128
R = 32


def block_scale(stream_key, extent, pieces, least, high):
    loudness = 1.0
    for position, blocks in pieces:
        steps = jax.random.uniform(jax.random.fold_in(jax.random.fold_in(stream_key, 6), position), (blocks,), jnp.float32, least / len(pieces), high / len(pieces))
        loudness = loudness * jnp.repeat(jnp.exp(steps), extent[position] // blocks).reshape((-1,) + (1,) * (len(extent) - 1 - position))
    return loudness


def centred(rng, extent, scale, bound, shards=(), kind=jnp.bfloat16):
    values = scale * jax.random.normal(rng, extent, jnp.float32)
    if shards:
        values = values * block_scale(rng, extent, shards, -0.22, 0.18)
    return jnp.clip(values, -bound, bound).astype(kind)


def setup_inputs(seed: int = 0, part: int = 0) -> dict:
    keys = jax.random.split(jax.random.key(seed), 6)
    part_splits = jax.random.split(jax.random.fold_in(keys[5], part), 6)
    left_act = centred(part_splits[0], (S, R, C), 1.0, 6.0, ((0, 4), (1, 4)), jnp.float32)
    right_act = centred(part_splits[1], (S, R, C), 1.0, 6.0, ((0, 4), (1, 4)), jnp.float32)
    weight = centred(keys[2], (C * C, Z), (C * C // 16) ** -0.5, 0.75, (), jnp.float32)
    bias = centred(keys[3], (Z,), 0.3, 1.8, (), jnp.float32)
    cotangent = centred(part_splits[4], (R, R, Z), 0.1, 0.6, ((0, 4), (1, 4)), jnp.float32)
    return {"left_act": left_act, "right_act": right_act, "weight": weight, "bias": bias, "cotangent": cotangent}


def block_terms(left_block, right_full, cot_block, weight_cube, bias):
    seqs = right_full.shape[0]
    highest = lax.Precision.HIGHEST
    products = jnp.einsum("sic,sjd->icjd", left_block, right_full, precision=highest) / seqs
    pair_block = jnp.einsum("icjd,cdz->ijz", products, weight_cube, precision=highest) + bias
    grad_outer = jnp.einsum("ijz,cdz->icjd", cot_block, weight_cube, precision=highest)
    weight_term = jnp.einsum("icjd,ijz->cdz", products, cot_block, precision=highest)
    left_term = jnp.einsum("icjd,sjd->sic", grad_outer, right_full, precision=highest) / seqs
    right_term = jnp.einsum("icjd,sic->sjd", grad_outer, left_block, precision=highest) / seqs
    return pair_block, weight_term, left_term, right_term


def reference(left_act, right_act, weight, bias, cotangent):
    residues = left_act.shape[1]
    width = left_act.shape[2]
    pair_width = weight.shape[1]
    block_rows = math.gcd(residues, 32)
    block_count = residues // block_rows
    weight_cube = weight.reshape(width, width, pair_width)

    def one_block(totals, block_index):
        start = (block_index * block_rows).astype(jnp.int32)
        left_block = lax.dynamic_slice_in_dim(left_act, start, block_rows, 1)
        cot_block = lax.dynamic_slice_in_dim(cotangent, start, block_rows, 0)
        pair_block, weight_term, left_term, right_term = block_terms(left_block, right_act, cot_block, weight_cube, bias)
        return (totals[0] + weight_term, totals[1] + right_term), (pair_block, left_term)

    initial = (jnp.zeros((width, width, pair_width), jnp.float32), jnp.zeros(right_act.shape, jnp.float32))
    (grad_cube, grad_right), (pair_blocks, left_blocks) = lax.scan(one_block, initial, jnp.arange(block_count, dtype=jnp.int32))
    pair = pair_blocks.reshape(residues, residues, pair_width)
    grad_left = jnp.transpose(left_blocks, (1, 0, 2, 3)).reshape(left_act.shape)
    return pair, grad_left, grad_right, grad_cube.reshape(width * width, pair_width)
```

```python
import functools

import jax
import jax.numpy as jnp
from jax import lax
from jax.experimental import pallas as pl
from jax.experimental.pallas import tpu as pltpu
from jax.sharding import PartitionSpec as P

LANES = 128
SUBLANES = 8
NN = (((1,), (0,)), ((), ()))
NT = (((1,), (1,)), ((), ()))


def split(value):
    high = value.astype(jnp.bfloat16)
    low = (value - high.astype(jnp.float32)).astype(jnp.bfloat16)
    return high, low


def product(a, b, dims):
    dot = functools.partial(lax.dot_general, dimension_numbers=dims, preferred_element_type=jnp.float32)
    return dot(a[0], b[1]) + dot(a[1], b[0]) + dot(a[0], b[0])


def swap_groups(tiles, width):
    lane = lax.broadcasted_iota(jnp.int32, tiles[0].shape, 1)
    low_half = lane < 2 * width
    even = lax.rem(lane // width, 2) == 0
    x = list(tiles)
    for p in (0, 1):
        a, b = x[p], x[p + 2]
        x[p] = jnp.where(low_half, a, pltpu.roll(b, 2 * width, 1))
        x[p + 2] = jnp.where(low_half, pltpu.roll(a, 2 * width, 1), b)
    for p in (0, 2):
        a, b = x[p], x[p + 1]
        x[p] = jnp.where(even, a, pltpu.roll(b, width, 1))
        x[p + 1] = jnp.where(even, pltpu.roll(a, LANES - width, 1), b)
    return x


def fused_kernel(
    n, seqs, left_count, right_count, width, pair_width,
    l_ref, r_ref, w_hbm, b_ref, c_ref,
    pair_ref, gl_ref, gr_ref, gw_ref,
    lpack, rpack, lbuf, rbuf, wv, ltr, o2, gop,
    gw, gwa, gwxs, gwx, gwzs, gwz, gwf, gwo, gls, grs, glb, grb,
    w_sem, rs_sem, rr_sem, ls_sem, lr_sem, as_sem, ar_sem, xs_sem, xr_sem,
    zs_sem, zr_sem, fs_sem, fr_sem, gls_sem, glr_sem, grs_sem, grr_sem,
):
    group, row, col = lax.axis_index("groups"), lax.axis_index("row"), lax.axis_index("col")
    share = seqs // n
    quads = LANES // width
    halves = right_count // quads
    blocks = width // quads
    core, side = lax.rem(col, 2), col // 2

    def remote(src, dst, send, recv, to_row, to_col):
        return pltpu.make_async_remote_copy(
            src_ref=src, dst_ref=dst, send_sem=send, recv_sem=recv,
            device_id=(group, to_row, to_col), device_id_type=pl.DeviceIdType.MESH,
        )

    barrier = pltpu.get_barrier_semaphore()
    for dr in range(n):
        for dc in range(n):
            if dr or dc:
                pl.semaphore_signal(
                    barrier, inc=1,
                    device_id=(group, lax.rem(row + dr, n), lax.rem(col + dc, n)),
                    device_id_type=pl.DeviceIdType.MESH,
                )
    w_copy = pltpu.make_async_copy(w_hbm, wv, w_sem)
    w_copy.start()

    for i in range(left_count):
        lpack[:, i * width:(i + 1) * width] = l_ref[pl.ds(i, share, stride=left_count), :]
    for j in range(right_count):
        rpack[:, j * width:(j + 1) * width] = r_ref[pl.ds(j, share, stride=right_count), :]
    pl.semaphore_wait(barrier, n * n - 1)

    sends = []
    for k in (2, 1, 3):
        to = lax.rem(row + k, n)
        sends.append(remote(rpack, rbuf.at[row], rs_sem.at[k - 1], rr_sem.at[row], to, col))
        sends.append(remote(lpack, lbuf.at[row], ls_sem.at[k], lr_sem.at[row], col, lax.rem(col + k, n)))
    for copy in sends:
        copy.start()
    pltpu.make_async_copy(rpack, rbuf.at[row], rr_sem.at[row]).start()
    diagonal = row == col
    l_own = remote(lpack, lbuf.at[row], ls_sem.at[0], lr_sem.at[row], col, col)

    @pl.when(diagonal)
    def _():
        pltpu.make_async_copy(lpack, lbuf.at[row], lr_sem.at[row]).start()

    @pl.when(jnp.logical_not(diagonal))
    def _():
        l_own.start()

    cot = jnp.concatenate(
        [c_ref[pl.ds(j, left_count, stride=right_count), :] for j in range(right_count)], axis=0
    )
    cot_parts = split(cot)
    w_copy.wait()
    w_parts = split(wv[...])
    go2 = product(cot_parts, w_parts, NT) * (1.0 / seqs)
    for h in range(halves):
        for q in range(blocks):
            tiles = [
                go2[(h * quads + b) * left_count:(h * quads + b + 1) * left_count, q * LANES:(q + 1) * LANES]
                for b in range(quads)
            ]
            for a, tile in enumerate(swap_groups(tiles, width)):
                at = (q * quads + a) * left_count
                gop[at:at + left_count, h * LANES:(h + 1) * LANES] = tile
    go_parts = split(gop[...])
    cot_t = split(cot.T)

    for k in range(n):
        pltpu.make_async_copy(rpack, rbuf.at[k], rr_sem.at[k]).wait()
    for k in range(n):
        pltpu.make_async_copy(lpack, lbuf.at[k], lr_sem.at[k]).wait()
    right = rbuf[...].reshape(seqs, right_count * width)
    right_parts = split(right)
    ltr[...] = lbuf[...].reshape(seqs, left_count * width).T
    left_t = jnp.concatenate(
        [ltr[pl.ds(c, left_count, stride=width), :] for c in range(width)], axis=0
    )
    outer = product(split(left_t), right_parts, NN) * (1.0 / seqs)
    for h in range(halves):
        for q in range(blocks):
            tiles = [
                outer[(q * quads + a) * left_count:(q * quads + a + 1) * left_count, h * LANES:(h + 1) * LANES]
                for a in range(quads)
            ]
            for b, tile in enumerate(swap_groups(tiles, width)):
                at = (h * quads + b) * left_count
                o2[at:at + left_count, q * LANES:(q + 1) * LANES] = tile
    outer_parts = split(o2[...])
    outer_t = split(o2[...].T)
    gw[...] = product(outer_t, cot_parts, NN).reshape(gw.shape)

    mate = 2 * side + (1 - core)
    across = 2 * (1 - side) + core
    far = remote(gw.at[:, 1 - side, 1 - core], gwa.at[:, 1 - side], as_sem.at[0], ar_sem.at[0], row, mate)
    near = remote(gw.at[:, side, 1 - core], gwa.at[:, side], as_sem.at[1], ar_sem.at[1], row, mate)
    far.start()
    near.start()
    sends += [far, near]

    grs[...] = product(split(left_t.T), go_parts, NN).reshape(grs.shape)
    for k in (2, 1, 3):
        to = lax.rem(row + k, n)
        copy = remote(grs.at[to], grb.at[row], grs_sem.at[k - 1], grr_sem.at[row], to, col)
        copy.start()
        sends.append(copy)
    glt = product(go_parts, right_parts, NT)
    for c in range(width):
        ltr[pl.ds(c, left_count, stride=width), :] = glt[c * left_count:(c + 1) * left_count, :]
    gls[...] = ltr[...].T.reshape(gls.shape)
    for k in (2, 1, 3):
        to = lax.rem(row + k, n)
        copy = remote(gls.at[to], glb.at[col], gls_sem.at[k], glr_sem.at[col], to, row)
        copy.start()
        sends.append(copy)
    gl_own = remote(gls.at[row], glb.at[col], gls_sem.at[0], glr_sem.at[col], row, row)

    @pl.when(diagonal)
    def _():
        pltpu.make_async_copy(gls.at[row], glb.at[col], glr_sem.at[col]).start()

    @pl.when(jnp.logical_not(diagonal))
    def _():
        gl_own.start()

    order = (2, 3, 1, 0)
    far.wait_recv()
    crossing = []
    for k in order:
        at = lax.rem(row + k, n)
        gwxs[at] = gw[at, 1 - side, core] + gwa[at, 1 - side]
        copy = remote(gwxs.at[at], gwx.at[at], xs_sem.at[k], xr_sem.at[at], row, across)
        copy.start()
        crossing.append(copy)
    sends += crossing
    near.wait_recv()

    pair = product(outer_parts, w_parts, NN) + b_ref[...]
    for j in range(right_count):
        pair_ref[pl.ds(j, left_count, stride=right_count), :] = pair[j * left_count:(j + 1) * left_count, :]

    total = None
    for k, copy in zip(order, crossing):
        at = lax.rem(row + k, n)
        copy.wait_recv()
        total = gw[at, side, core] + gwa[at, side] + gwx[at]
        if k:
            gwzs[k - 1] = total
            out = remote(gwzs.at[k - 1], gwz.at[row], zs_sem.at[k - 1], zr_sem.at[row], at, col)
            out.start()
            sends.append(out)

    for k in range(1, n):
        at = lax.rem(row + k, n)
        pltpu.make_async_copy(grs.at[at], grb.at[at], grr_sem.at[at]).wait()
    gr_sum = grs[row]
    for k in range(1, n):
        gr_sum += grb[lax.rem(row + k, n)]
    for j in range(right_count):
        gr_ref[pl.ds(j, share, stride=right_count), :] = gr_sum[:, j * width:(j + 1) * width]
    for k in range(n):
        pltpu.make_async_copy(gls.at[k], glb.at[k], glr_sem.at[k]).wait()
    gl_sum = glb[0]
    for k in range(1, n):
        gl_sum += glb[k]
    for i in range(left_count):
        gl_ref[pl.ds(i, share, stride=left_count), :] = gl_sum[:, i * width:(i + 1) * width]

    for k in range(1, n):
        at = lax.rem(row + k, n)
        pltpu.make_async_copy(gwf, gwz.at[at], zr_sem.at[at]).wait()
        total += gwz[at]
    gwf[...] = total
    for k in (2, 3, 1):
        copy = remote(gwf, gwo.at[col], fs_sem.at[k - 1], fr_sem.at[col], row, lax.rem(col + k, n))
        copy.start()
        sends.append(copy)
    piece = total.shape[0]
    gw_ref[pl.ds(pl.multiple_of(col * piece, piece), piece), :] = total
    for k in (1, 2, 3):
        at = lax.rem(col + k, n)
        pltpu.make_async_copy(gwf, gwo.at[at], fr_sem.at[at]).wait()
        gw_ref[pl.ds(pl.multiple_of(at * piece, piece), piece), :] = gwo[at]

    for copy in sends:
        copy.wait_send()

    @pl.when(jnp.logical_not(diagonal))
    def _():
        l_own.wait_send()
        gl_own.wait_send()


def fused(n, left_act, right_act, weight, bias, cotangent):
    share, right_count, width = right_act.shape
    left_count = cotangent.shape[0]
    pair_width = weight.shape[1]
    seqs = share * n
    f32 = jnp.float32
    left_lanes, right_lanes = left_count * width, right_count * width
    piece = width * width // (n * n)
    dma = pltpu.SemaphoreType.DMA
    vmem = pl.BlockSpec(memory_space=pltpu.VMEM)
    shape = jax.ShapeDtypeStruct
    pair, gl, gr, gw = pl.pallas_call(
        functools.partial(fused_kernel, n, seqs, left_count, right_count, width, pair_width),
        out_shape=(
            shape((left_count * right_count, pair_width), f32),
            shape((share * left_count, width), f32),
            shape((share * right_count, width), f32),
            shape((width * width // n, pair_width), f32),
        ),
        in_specs=[vmem, vmem, pl.BlockSpec(memory_space=pl.ANY), vmem, vmem],
        out_specs=(vmem, vmem, vmem, vmem),
        scratch_shapes=[
            pltpu.VMEM((share, left_lanes), f32),
            pltpu.VMEM((share, right_lanes), f32),
            pltpu.VMEM((n, share, left_lanes), f32),
            pltpu.VMEM((n, share, right_lanes), f32),
            pltpu.VMEM(weight.shape, f32),
            pltpu.VMEM((left_lanes, seqs), f32),
            pltpu.VMEM((left_count * right_count, width * width), f32),
            pltpu.VMEM((left_lanes, right_lanes), f32),
            pltpu.VMEM((n, 2, 2, piece, pair_width), f32),
            pltpu.VMEM((n, 2, piece, pair_width), f32),
            pltpu.VMEM((n, piece, pair_width), f32),
            pltpu.VMEM((n, piece, pair_width), f32),
            pltpu.VMEM((n - 1, piece, pair_width), f32),
            pltpu.VMEM((n, piece, pair_width), f32),
            pltpu.VMEM((piece, pair_width), f32),
            pltpu.VMEM((n, piece, pair_width), f32),
            pltpu.VMEM((n, share, left_lanes), f32),
            pltpu.VMEM((n, share, right_lanes), f32),
            pltpu.VMEM((n, share, left_lanes), f32),
            pltpu.VMEM((n, share, right_lanes), f32),
            dma(()),
            dma((n - 1,)), dma((n,)), dma((n,)), dma((n,)),
            dma((2,)), dma((2,)), dma((n,)), dma((n,)),
            dma((n - 1,)), dma((n,)), dma((n - 1,)), dma((n,)),
            dma((n,)), dma((n,)), dma((n - 1,)), dma((n,)),
        ],
        compiler_params=pltpu.CompilerParams(collective_id=0, has_side_effects=True),
    )(
        left_act.reshape(share * right_count, width),
        right_act.reshape(share * right_count, width),
        weight,
        bias.reshape(1, pair_width),
        cotangent.reshape(left_count * right_count, pair_width),
    )
    return (
        pair.reshape(cotangent.shape),
        gl.reshape(left_act.shape),
        gr.reshape(right_act.shape),
        gw,
    )


def block_terms(left_block, right_full, cot_block, weight_cube, bias):
    seqs = right_full.shape[0]
    highest = lax.Precision.HIGHEST
    products = jnp.einsum("sic,sjd->icjd", left_block, right_full, precision=highest) / seqs
    pair_block = jnp.einsum("icjd,cdz->ijz", products, weight_cube, precision=highest) + bias
    grad_outer = jnp.einsum("ijz,cdz->icjd", cot_block, weight_cube, precision=highest)
    weight_term = jnp.einsum("icjd,ijz->cdz", products, cot_block, precision=highest)
    left_term = jnp.einsum("icjd,sjd->sic", grad_outer, right_full, precision=highest) / seqs
    right_term = jnp.einsum("icjd,sic->sjd", grad_outer, left_block, precision=highest) / seqs
    return (pair_block, weight_term, left_term, right_term)


def general(left_act, right_act, weight, bias, cotangent):
    width = left_act.shape[2]
    pair_width = weight.shape[1]
    widened = lax.all_gather(left_act, "col", axis=1, tiled=True)
    left_full = lax.all_to_all(widened, "row", split_axis=1, concat_axis=0, tiled=True)
    right_full = lax.all_gather(right_act, "row", axis=0, tiled=True)
    weight_cube = weight.reshape(width, width, pair_width)
    pair, grad_cube, left_partial, right_partial = block_terms(
        left_full, right_full, cotangent, weight_cube, bias
    )
    returned = lax.all_to_all(left_partial, "row", split_axis=0, concat_axis=1, tiled=True)
    grad_left = lax.psum_scatter(returned, "col", scatter_dimension=1, tiled=True)
    grad_right = lax.psum_scatter(right_partial, "row", scatter_dimension=0, tiled=True)
    grad_flat = grad_cube.reshape(width * width, pair_width)
    weight_part = lax.psum_scatter(grad_flat, "row", scatter_dimension=0, tiled=True)
    grad_weight = lax.psum(weight_part, "col")
    return (pair, grad_left, grad_right, grad_weight)


def shards(rows, cols, left_act, right_act, weight, bias, cotangent):
    share, right_count, width = right_act.shape
    left_count = cotangent.shape[0]
    fits = (
        rows == cols == 4
        and left_count == right_count == SUBLANES
        and share % SUBLANES == 0
        and share * rows == LANES
        and 4 * width == LANES
        and weight.shape[1] == LANES
    )
    if fits:
        return fused(rows, left_act, right_act, weight, bias, cotangent)
    return general(left_act, right_act, weight, bias, cotangent)


def solution(mesh):
    placed = (
        P(("groups", "row"), "col", None),
        P(("groups", "row"), "col", None),
        P(),
        P(),
        P(("groups", "row"), "col", None),
    )
    return jax.shard_map(
        functools.partial(shards, mesh.shape["row"], mesh.shape["col"]),
        mesh=mesh,
        in_specs=placed,
        out_specs=(
            P(("groups", "row"), "col", None),
            P(("groups", "row"), "col", None),
            P(("groups", "row"), "col", None),
            P(("groups", "row"), None),
        ),
        check_vma=False,
    )
```

```python
import functools

import jax
import jax.numpy as jnp
from jax import lax
from jax.experimental import pallas as pl
from jax.experimental.pallas import tpu as pltpu
from jax.sharding import PartitionSpec as P

LANES = 128
SUBLANES = 8
NN = (((1,), (0,)), ((), ()))
NT = (((1,), (1,)), ((), ()))


def split(value):
    high = value.astype(jnp.bfloat16)
    low = (value - high.astype(jnp.float32)).astype(jnp.bfloat16)
    return high, low


def product(a, b, dims):
    dot = functools.partial(lax.dot_general, dimension_numbers=dims, preferred_element_type=jnp.float32)
    return dot(a[0], b[1]) + dot(a[1], b[0]) + dot(a[0], b[0])


def swap_groups(tiles, width):
    lane = lax.broadcasted_iota(jnp.int32, tiles[0].shape, 1)
    low_half = lane < 2 * width
    even = lax.rem(lane // width, 2) == 0
    x = list(tiles)
    for p in (0, 1):
        a, b = x[p], x[p + 2]
        x[p] = jnp.where(low_half, a, pltpu.roll(b, 2 * width, 1))
        x[p + 2] = jnp.where(low_half, pltpu.roll(a, 2 * width, 1), b)
    for p in (0, 2):
        a, b = x[p], x[p + 1]
        x[p] = jnp.where(even, a, pltpu.roll(b, width, 1))
        x[p + 1] = jnp.where(even, pltpu.roll(a, LANES - width, 1), b)
    return x


def fused_kernel(
    n, seqs, left_count, right_count, width,
    l_hbm, r_hbm, w_hbm, b_ref, c_hbm,
    pair_ref, gl_ref, gr_ref, gw_ref,
    l_in, r_in, wv, lpack, rpack, lbuf, rbuf, call, ltr, rtr, rsl, rq, o2, oq, gop,
    gws, gwz, gwf, gwo, gls, glc, gln, glf, grs, grb,
    in_sem, rs_sem, rr_sem, ls_sem, lr_sem, lf_sem, cs_sem, cr_sem, qs_sem, qr_sem,
    gs_sem, gr_sem, fs_sem, fr_sem, g1_sem, g1r_sem, g2_sem, g2r_sem, h_sem, hr_sem,
):
    group, row, col = lax.axis_index("groups"), lax.axis_index("row"), lax.axis_index("col")
    share = seqs // n
    quads = LANES // width
    halves = right_count // quads
    blocks = width // quads
    slice_width = width // n
    seq_scale = 1.0 / seqs

    def remote(src, dst, send, recv, to_row, to_col):
        return pltpu.make_async_remote_copy(
            src_ref=src, dst_ref=dst, send_sem=send, recv_sem=recv,
            device_id=(group, to_row, to_col), device_id_type=pl.DeviceIdType.MESH,
        )

    def row_at(k):
        return lax.rem(row + k, n)

    def col_at(k):
        return lax.rem(col + k, n)

    barrier = pltpu.get_barrier_semaphore()
    for dr in range(n):
        for dc in range(n):
            if dr or dc:
                pl.semaphore_signal(
                    barrier, inc=1, device_id=(group, row_at(dr), col_at(dc)),
                    device_id_type=pl.DeviceIdType.MESH,
                )
    fetches = [
        pltpu.make_async_copy(src, dst, in_sem.at[k])
        for k, (src, dst) in enumerate(
            ((l_hbm, l_in), (r_hbm, r_in), (c_hbm, call.at[col]), (w_hbm, wv))
        )
    ]
    for fetch in fetches:
        fetch.start()
    fetches[0].wait()
    for i in range(left_count):
        lpack[:, i * width:(i + 1) * width] = l_in[pl.ds(i, share, stride=left_count), :]
    fetches[1].wait()
    for j in range(right_count):
        rpack[:, j * width:(j + 1) * width] = r_in[pl.ds(j, share, stride=right_count), :]
    rbuf[row] = rpack[...]
    fetches[2].wait()
    pl.semaphore_wait(barrier, n * n - 1)

    sends = []

    def send(copy):
        copy.start()
        sends.append(copy)

    diagonal = row == col
    l_out = remote(lpack, lbuf.at[row], ls_sem, lr_sem.at[row], col, row)

    @pl.when(diagonal)
    def _():
        pltpu.make_async_copy(lpack, lbuf.at[row], lr_sem.at[row]).start()

    @pl.when(jnp.logical_not(diagonal))
    def _():
        l_out.start()

    for k in (2, 1, 3):
        send(remote(rpack, rbuf.at[row], rs_sem.at[k - 1], rr_sem.at[row], row_at(k), col))
    for k in (2, 1, 3):
        send(remote(call.at[col], call.at[col], cs_sem.at[k - 1], cr_sem.at[col], row, col_at(k)))

    cot = jnp.concatenate(
        [call[col, pl.ds(j, left_count, stride=right_count), :] for j in range(right_count)], axis=0
    )
    fetches[3].wait()
    w_parts = split(wv[...])
    go2 = product(split(cot), w_parts, NT) * seq_scale
    for h in range(halves):
        for q in range(blocks):
            tiles = [
                go2[(h * quads + b) * left_count:(h * quads + b + 1) * left_count, q * LANES:(q + 1) * LANES]
                for b in range(quads)
            ]
            for a, tile in enumerate(swap_groups(tiles, width)):
                at = (q * quads + a) * left_count
                gop[at:at + left_count, h * LANES:(h + 1) * LANES] = tile
    go_parts = split(gop[...])

    pltpu.make_async_copy(lpack, lbuf.at[col], lr_sem.at[col]).wait()
    for k in (2, 1, 3):
        send(remote(lbuf.at[col], lbuf.at[col], lf_sem.at[k - 1], lr_sem.at[col], row, col_at(k)))
    for k in range(1, n):
        pltpu.make_async_copy(rpack, rbuf.at[row_at(k)], rr_sem.at[row_at(k)]).wait()
    right = rbuf[...].reshape(seqs, right_count * width)
    rtr[...] = right.T
    for d in range(width):
        at = d % slice_width * right_count
        rsl[d // slice_width, at:at + right_count, :] = rtr[pl.ds(d, right_count, stride=width), :]
    for k in (2, 1, 3):
        send(remote(rsl.at[col_at(k)], rq.at[col], qs_sem.at[k - 1], qr_sem.at[col], row, col_at(k)))
    rq[col] = rsl[col]

    right_parts = split(right)
    glt = product(go_parts, right_parts, NT)
    for c in range(width):
        ltr[pl.ds(c, left_count, stride=width), :] = glt[c * left_count:(c + 1) * left_count, :]
    gls[...] = ltr[...].T.reshape(gls.shape)
    for k in (2, 1, 3):
        send(remote(gls.at[col_at(k)], glc.at[col], g1_sem.at[k - 1], g1r_sem.at[col], row, col_at(k)))

    for k in range(1, n):
        pltpu.make_async_copy(lpack, lbuf.at[col_at(k)], lr_sem.at[col_at(k)]).wait()
    left = lbuf[...].reshape(seqs, left_count * width)
    left_parts = split(left)
    for k in range(1, n):
        pltpu.make_async_copy(rsl.at[col], rq.at[col_at(k)], qr_sem.at[col_at(k)]).wait()
    slice_t = jnp.concatenate(
        [
            rq[k, d * right_count:(d + 1) * right_count, :]
            for d in range(slice_width)
            for k in range(n)
        ],
        axis=0,
    )
    outer_q = product(split(slice_t), left_parts, NN) * seq_scale
    span = n * right_count
    for h in range(left_count // quads):
        for q in range(slice_width // quads):
            tiles = [
                outer_q[(q * quads + a) * span:(q * quads + a + 1) * span, h * LANES:(h + 1) * LANES]
                for a in range(quads)
            ]
            for b, tile in enumerate(swap_groups(tiles, width)):
                at = (h * quads + b) * span
                oq[at:at + span, q * LANES:(q + 1) * LANES] = tile
    for k in range(1, n):
        pltpu.make_async_copy(call.at[col], call.at[col_at(k)], cr_sem.at[col_at(k)]).wait()
    cot_all = jnp.concatenate(
        [
            call[k, i * right_count:(i + 1) * right_count, :]
            for i in range(left_count)
            for k in range(n)
        ],
        axis=0,
    )
    gws[...] = product(split(oq[...].T), split(cot_all), NN).reshape(gws.shape)
    for k in (2, 1, 3):
        send(remote(gws.at[:, row_at(k)], gwz.at[row], gs_sem.at[k - 1], gr_sem.at[row], row_at(k), col))

    ltr[...] = left.T
    left_t = jnp.concatenate(
        [ltr[pl.ds(c, left_count, stride=width), :] for c in range(width)], axis=0
    )
    grs[...] = product(split(left_t.T), go_parts, NN).reshape(grs.shape)
    for k in (2, 1, 3):
        send(remote(grs.at[row_at(k)], grb.at[row], h_sem.at[k - 1], hr_sem.at[row], row_at(k), col))

    for k in range(1, n):
        pltpu.make_async_copy(gls.at[col], glc.at[col_at(k)], g1r_sem.at[col_at(k)]).wait()
    gl_sum = gls[col]
    for k in range(1, n):
        gl_sum += glc[col_at(k)]
    gln[...] = gl_sum
    gl_out = remote(gln, glf, g2_sem, g2r_sem, col, row)

    @pl.when(diagonal)
    def _():
        pltpu.make_async_copy(gln, glf, g2r_sem).start()

    @pl.when(jnp.logical_not(diagonal))
    def _():
        gl_out.start()

    outer = product(split(left_t), right_parts, NN) * seq_scale
    for h in range(halves):
        for q in range(blocks):
            tiles = [
                outer[(q * quads + a) * left_count:(q * quads + a + 1) * left_count, h * LANES:(h + 1) * LANES]
                for a in range(quads)
            ]
            for b, tile in enumerate(swap_groups(tiles, width)):
                at = (h * quads + b) * left_count
                o2[at:at + left_count, q * LANES:(q + 1) * LANES] = tile
    pair = product(split(o2[...]), w_parts, NN) + b_ref[...]
    for j in range(right_count):
        pair_ref[pl.ds(j, left_count, stride=right_count), :] = pair[j * left_count:(j + 1) * left_count, :]

    total = gws[:, row]
    for k in range(1, n):
        at = row_at(k)
        pltpu.make_async_copy(gws.at[:, at], gwz.at[at], gr_sem.at[at]).wait()
        total += gwz[at]
    gwf[...] = total
    gwo[col] = total
    for k in (2, 3, 1):
        send(remote(gwf, gwo.at[col], fs_sem.at[k - 1], fr_sem.at[col], row, col_at(k)))
    gr_sum = grs[row]
    for k in range(1, n):
        at = row_at(k)
        pltpu.make_async_copy(grs.at[at], grb.at[at], hr_sem.at[at]).wait()
        gr_sum += grb[at]
    for j in range(right_count):
        gr_ref[pl.ds(j, share, stride=right_count), :] = gr_sum[:, j * width:(j + 1) * width]
    pltpu.make_async_copy(gln, glf, g2r_sem).wait()
    gl_own = glf[...]
    for i in range(left_count):
        gl_ref[pl.ds(i, share, stride=left_count), :] = gl_own[:, i * width:(i + 1) * width]
    for k in range(1, n):
        at = col_at(k)
        pltpu.make_async_copy(gwf, gwo.at[at], fr_sem.at[at]).wait()
    for k in range(n):
        for d in range(slice_width):
            gw_ref[pl.ds(k * slice_width + d, width // n, stride=width), :] = gwo[k, d]

    for copy in sends:
        copy.wait_send()

    @pl.when(jnp.logical_not(diagonal))
    def _():
        l_out.wait_send()
        gl_out.wait_send()


def fused(n, left_act, right_act, weight, bias, cotangent):
    share, right_count, width = right_act.shape
    left_count = cotangent.shape[0]
    pair_width = weight.shape[1]
    seqs = share * n
    f32 = jnp.float32
    left_lanes, right_lanes = left_count * width, right_count * width
    pairs = left_count * right_count
    slice_width = width // n
    dma = pltpu.SemaphoreType.DMA
    anywhere = pl.BlockSpec(memory_space=pl.ANY)
    vmem = pl.BlockSpec(memory_space=pltpu.VMEM)
    shapes = (
        (pairs, pair_width),
        (share * left_count, width),
        (share * right_count, width),
        (width * width // n, pair_width),
    )
    pair, gl, gr, gw = pl.pallas_call(
        functools.partial(fused_kernel, n, seqs, left_count, right_count, width),
        out_shape=tuple(pltpu.VMEM(shape, f32) for shape in shapes),
        in_specs=[anywhere, anywhere, anywhere, vmem, anywhere],
        out_specs=(vmem,) * len(shapes),
        scratch_shapes=[
            pltpu.VMEM((share * left_count, width), f32),
            pltpu.VMEM((share * right_count, width), f32),
            pltpu.VMEM(weight.shape, f32),
            pltpu.VMEM((share, left_lanes), f32),
            pltpu.VMEM((share, right_lanes), f32),
            pltpu.VMEM((n, share, left_lanes), f32),
            pltpu.VMEM((n, share, right_lanes), f32),
            pltpu.VMEM((n, pairs, pair_width), f32),
            pltpu.VMEM((left_lanes, seqs), f32),
            pltpu.VMEM((right_lanes, seqs), f32),
            pltpu.VMEM((n, right_count * slice_width, seqs), f32),
            pltpu.VMEM((n, right_count * slice_width, seqs), f32),
            pltpu.VMEM((pairs, width * width), f32),
            pltpu.VMEM((left_count * right_count * n, slice_width * width), f32),
            pltpu.VMEM((left_lanes, right_lanes), f32),
            pltpu.VMEM((slice_width, n, width // n, pair_width), f32),
            pltpu.VMEM((n, slice_width, width // n, pair_width), f32),
            pltpu.VMEM((slice_width, width // n, pair_width), f32),
            pltpu.VMEM((n, slice_width, width // n, pair_width), f32),
            pltpu.VMEM((n, share, left_lanes), f32),
            pltpu.VMEM((n, share, left_lanes), f32),
            pltpu.VMEM((share, left_lanes), f32),
            pltpu.VMEM((share, left_lanes), f32),
            pltpu.VMEM((n, share, right_lanes), f32),
            pltpu.VMEM((n, share, right_lanes), f32),
            dma((4,)), dma((n - 1,)), dma((n,)), dma(()), dma((n,)), dma((n - 1,)),
            dma((n - 1,)), dma((n,)), dma((n - 1,)), dma((n,)),
            dma((n - 1,)), dma((n,)), dma((n - 1,)), dma((n,)),
            dma((n - 1,)), dma((n,)), dma(()), dma(()), dma((n - 1,)), dma((n,)),
        ],
        compiler_params=pltpu.CompilerParams(collective_id=0, has_side_effects=True),
    )(
        left_act.reshape(share * right_count, width),
        right_act.reshape(share * right_count, width),
        weight,
        bias.reshape(1, pair_width),
        cotangent.reshape(pairs, pair_width),
    )
    return (
        pair.reshape(cotangent.shape),
        gl.reshape(left_act.shape),
        gr.reshape(right_act.shape),
        gw,
    )


def block_terms(left_block, right_full, cot_block, weight_cube, bias):
    seqs = right_full.shape[0]
    highest = lax.Precision.HIGHEST
    products = jnp.einsum("sic,sjd->icjd", left_block, right_full, precision=highest) / seqs
    pair_block = jnp.einsum("icjd,cdz->ijz", products, weight_cube, precision=highest) + bias
    grad_outer = jnp.einsum("ijz,cdz->icjd", cot_block, weight_cube, precision=highest)
    weight_term = jnp.einsum("icjd,ijz->cdz", products, cot_block, precision=highest)
    left_term = jnp.einsum("icjd,sjd->sic", grad_outer, right_full, precision=highest) / seqs
    right_term = jnp.einsum("icjd,sic->sjd", grad_outer, left_block, precision=highest) / seqs
    return (pair_block, weight_term, left_term, right_term)


def general(left_act, right_act, weight, bias, cotangent):
    width = left_act.shape[2]
    pair_width = weight.shape[1]
    widened = lax.all_gather(left_act, "col", axis=1, tiled=True)
    left_full = lax.all_to_all(widened, "row", split_axis=1, concat_axis=0, tiled=True)
    right_full = lax.all_gather(right_act, "row", axis=0, tiled=True)
    weight_cube = weight.reshape(width, width, pair_width)
    pair, grad_cube, left_partial, right_partial = block_terms(
        left_full, right_full, cotangent, weight_cube, bias
    )
    returned = lax.all_to_all(left_partial, "row", split_axis=0, concat_axis=1, tiled=True)
    grad_left = lax.psum_scatter(returned, "col", scatter_dimension=1, tiled=True)
    grad_right = lax.psum_scatter(right_partial, "row", scatter_dimension=0, tiled=True)
    grad_flat = grad_cube.reshape(width * width, pair_width)
    weight_part = lax.psum_scatter(grad_flat, "row", scatter_dimension=0, tiled=True)
    grad_weight = lax.psum(weight_part, "col")
    return (pair, grad_left, grad_right, grad_weight)


def shards(rows, cols, left_act, right_act, weight, bias, cotangent):
    share, right_count, width = right_act.shape
    left_count = cotangent.shape[0]
    fits = (
        rows == cols == 4
        and left_count == right_count == SUBLANES
        and share % SUBLANES == 0
        and share * rows == LANES
        and 4 * width == LANES
        and weight.shape[1] == LANES
    )
    if fits:
        return fused(rows, left_act, right_act, weight, bias, cotangent)
    return general(left_act, right_act, weight, bias, cotangent)


def solution(mesh):
    placed = (
        P(("groups", "row"), "col", None),
        P(("groups", "row"), "col", None),
        P(),
        P(),
        P(("groups", "row"), "col", None),
    )
    return jax.shard_map(
        functools.partial(shards, mesh.shape["row"], mesh.shape["col"]),
        mesh=mesh,
        in_specs=placed,
        out_specs=(
            P(("groups", "row"), "col", None),
            P(("groups", "row"), "col", None),
            P(("groups", "row"), "col", None),
            P(("groups", "row"), None),
        ),
        check_vma=False,
    )
```

```python
import functools

import jax
import jax.numpy as jnp
from jax import lax
from jax.experimental import pallas as pl
from jax.experimental.pallas import tpu as pltpu
from jax.sharding import PartitionSpec as P

LANES = 128
SUBLANES = 8
NN = (((1,), (0,)), ((), ()))
NT = (((1,), (1,)), ((), ()))


def split(value):
    high = value.astype(jnp.bfloat16)
    low = (value - high.astype(jnp.float32)).astype(jnp.bfloat16)
    return high, low


def product(a, b, dims):
    dot = functools.partial(lax.dot_general, dimension_numbers=dims, preferred_element_type=jnp.float32)
    return dot(a[0], b[1]) + dot(a[1], b[0]) + dot(a[0], b[0])


def swap_groups(tiles, width):
    lane = lax.broadcasted_iota(jnp.int32, tiles[0].shape, 1)
    low_half = lane < 2 * width
    even = lax.rem(lane // width, 2) == 0
    x = list(tiles)
    for p in (0, 1):
        a, b = x[p], x[p + 2]
        x[p] = jnp.where(low_half, a, pltpu.roll(b, 2 * width, 1))
        x[p + 2] = jnp.where(low_half, pltpu.roll(a, 2 * width, 1), b)
    for p in (0, 2):
        a, b = x[p], x[p + 1]
        x[p] = jnp.where(even, a, pltpu.roll(b, width, 1))
        x[p + 1] = jnp.where(even, pltpu.roll(a, LANES - width, 1), b)
    return x


def fused_kernel(
    n, seqs, left_count, right_count, width,
    l_hbm, r_hbm, w_hbm, b_ref, c_hbm,
    pair_ref, gl_ref, gr_ref, gw_ref,
    l_in, r_in, wv, lpack, rpack, lbuf, rbuf, call, ltr, rtr, rsl, rq, o2, oq, gop,
    gws, gwz, gwf, gwo, gls, glc, gln, glf, grs, grb,
    in_sem, rs_sem, rr_sem, ls_sem, lr_sem, lf_sem, cs_sem, cr_sem, qs_sem, qr_sem,
    gs_sem, gr_sem, fs_sem, fr_sem, g1_sem, g1r_sem, g2_sem, g2r_sem, h_sem, hr_sem,
):
    group, row, col = lax.axis_index("groups"), lax.axis_index("row"), lax.axis_index("col")
    share = seqs // n
    quads = LANES // width
    halves = right_count // quads
    blocks = width // quads
    slice_width = width // n
    seq_scale = 1.0 / seqs

    def remote(src, dst, send, recv, to_row, to_col):
        return pltpu.make_async_remote_copy(
            src_ref=src, dst_ref=dst, send_sem=send, recv_sem=recv,
            device_id=(group, to_row, to_col), device_id_type=pl.DeviceIdType.MESH,
        )

    def row_at(k):
        return lax.rem(row + k, n)

    def col_at(k):
        return lax.rem(col + k, n)

    barrier = pltpu.get_barrier_semaphore()
    for dr in range(n):
        for dc in range(n):
            if dr or dc:
                pl.semaphore_signal(
                    barrier, inc=1, device_id=(group, row_at(dr), col_at(dc)),
                    device_id_type=pl.DeviceIdType.MESH,
                )
    fetches = [
        pltpu.make_async_copy(src, dst, in_sem.at[k])
        for k, (src, dst) in enumerate(
            ((l_hbm, l_in), (r_hbm, r_in), (c_hbm, call.at[col]), (w_hbm, wv))
        )
    ]
    for fetch in fetches:
        fetch.start()
    fetches[0].wait()
    for i in range(left_count):
        lpack[:, i * width:(i + 1) * width] = l_in[pl.ds(i, share, stride=left_count), :]
    fetches[1].wait()
    for j in range(right_count):
        rpack[:, j * width:(j + 1) * width] = r_in[pl.ds(j, share, stride=right_count), :]
    rbuf[row] = rpack[...]
    fetches[2].wait()
    pl.semaphore_wait(barrier, n * n - 1)

    sends = []

    def send(copy):
        copy.start()
        sends.append(copy)

    diagonal = row == col
    l_out = remote(lpack, lbuf.at[row], ls_sem, lr_sem.at[row], col, row)

    @pl.when(diagonal)
    def _():
        pltpu.make_async_copy(lpack, lbuf.at[row], lr_sem.at[row]).start()

    @pl.when(jnp.logical_not(diagonal))
    def _():
        l_out.start()

    for k in (2, 1, 3):
        send(remote(rpack, rbuf.at[row], rs_sem.at[k - 1], rr_sem.at[row], row_at(k), col))
    for k in (2, 1, 3):
        send(remote(call.at[col], call.at[col], cs_sem.at[k - 1], cr_sem.at[col], row, col_at(k)))

    cot = jnp.concatenate(
        [call[col, pl.ds(j, left_count, stride=right_count), :] for j in range(right_count)], axis=0
    )
    fetches[3].wait()
    w_parts = split(wv[...])
    go2 = product(split(cot), w_parts, NT) * seq_scale
    for h in range(halves):
        for q in range(blocks):
            tiles = [
                go2[(h * quads + b) * left_count:(h * quads + b + 1) * left_count, q * LANES:(q + 1) * LANES]
                for b in range(quads)
            ]
            for a, tile in enumerate(swap_groups(tiles, width)):
                at = (q * quads + a) * left_count
                gop[at:at + left_count, h * LANES:(h + 1) * LANES] = tile
    go_parts = split(gop[...])

    pltpu.make_async_copy(lpack, lbuf.at[col], lr_sem.at[col]).wait()
    for k in (2, 1, 3):
        send(remote(lbuf.at[col], lbuf.at[col], lf_sem.at[k - 1], lr_sem.at[col], row, col_at(k)))
    for k in range(1, n):
        pltpu.make_async_copy(rpack, rbuf.at[row_at(k)], rr_sem.at[row_at(k)]).wait()
    right = rbuf[...].reshape(seqs, right_count * width)
    rtr[...] = right.T
    for d in range(width):
        at = d % slice_width * right_count
        rsl[d // slice_width, at:at + right_count, :] = rtr[pl.ds(d, right_count, stride=width), :]
    for k in (2, 1, 3):
        send(remote(rsl.at[col_at(k)], rq.at[col], qs_sem.at[k - 1], qr_sem.at[col], row, col_at(k)))
    rq[col] = rsl[col]

    right_parts = split(right)
    glt = product(go_parts, right_parts, NT)
    for c in range(width):
        ltr[pl.ds(c, left_count, stride=width), :] = glt[c * left_count:(c + 1) * left_count, :]
    gls[...] = ltr[...].T.reshape(gls.shape)
    for k in (2, 1, 3):
        send(remote(gls.at[col_at(k)], glc.at[col], g1_sem.at[k - 1], g1r_sem.at[col], row, col_at(k)))

    for k in range(1, n):
        pltpu.make_async_copy(lpack, lbuf.at[col_at(k)], lr_sem.at[col_at(k)]).wait()
    left = lbuf[...].reshape(seqs, left_count * width)
    left_parts = split(left)
    for k in range(1, n):
        pltpu.make_async_copy(rsl.at[col], rq.at[col_at(k)], qr_sem.at[col_at(k)]).wait()
    slice_t = jnp.concatenate(
        [
            rq[k, d * right_count:(d + 1) * right_count, :]
            for d in range(slice_width)
            for k in range(n)
        ],
        axis=0,
    )
    outer_q = product(split(slice_t), left_parts, NN) * seq_scale
    span = n * right_count
    for h in range(left_count // quads):
        for q in range(slice_width // quads):
            tiles = [
                outer_q[(q * quads + a) * span:(q * quads + a + 1) * span, h * LANES:(h + 1) * LANES]
                for a in range(quads)
            ]
            for b, tile in enumerate(swap_groups(tiles, width)):
                at = (h * quads + b) * span
                oq[at:at + span, q * LANES:(q + 1) * LANES] = tile
    for k in range(1, n):
        pltpu.make_async_copy(call.at[col], call.at[col_at(k)], cr_sem.at[col_at(k)]).wait()
    cot_all = jnp.concatenate(
        [
            call[k, i * right_count:(i + 1) * right_count, :]
            for i in range(left_count)
            for k in range(n)
        ],
        axis=0,
    )
    gws[...] = product(split(oq[...].T), split(cot_all), NN).reshape(gws.shape)
    for k in (2, 1, 3):
        send(remote(gws.at[:, row_at(k)], gwz.at[row], gs_sem.at[k - 1], gr_sem.at[row], row_at(k), col))

    ltr[...] = left.T
    left_t = jnp.concatenate(
        [ltr[pl.ds(c, left_count, stride=width), :] for c in range(width)], axis=0
    )
    grs[...] = product(split(left_t.T), go_parts, NN).reshape(grs.shape)
    for k in (2, 1, 3):
        send(remote(grs.at[row_at(k)], grb.at[row], h_sem.at[k - 1], hr_sem.at[row], row_at(k), col))

    for k in range(1, n):
        pltpu.make_async_copy(gls.at[col], glc.at[col_at(k)], g1r_sem.at[col_at(k)]).wait()
    gl_sum = gls[col]
    for k in range(1, n):
        gl_sum += glc[col_at(k)]
    gln[...] = gl_sum
    gl_out = remote(gln, glf, g2_sem, g2r_sem, col, row)

    @pl.when(diagonal)
    def _():
        pltpu.make_async_copy(gln, glf, g2r_sem).start()

    @pl.when(jnp.logical_not(diagonal))
    def _():
        gl_out.start()

    outer = product(split(left_t), right_parts, NN) * seq_scale
    for h in range(halves):
        for q in range(blocks):
            tiles = [
                outer[(q * quads + a) * left_count:(q * quads + a + 1) * left_count, h * LANES:(h + 1) * LANES]
                for a in range(quads)
            ]
            for b, tile in enumerate(swap_groups(tiles, width)):
                at = (h * quads + b) * left_count
                o2[at:at + left_count, q * LANES:(q + 1) * LANES] = tile
    pair = product(split(o2[...]), w_parts, NN) + b_ref[...]
    for j in range(right_count):
        pair_ref[pl.ds(j, left_count, stride=right_count), :] = pair[j * left_count:(j + 1) * left_count, :]

    total = gws[:, row]
    for k in range(1, n):
        at = row_at(k)
        pltpu.make_async_copy(gws.at[:, at], gwz.at[at], gr_sem.at[at]).wait()
        total += gwz[at]
    gwf[...] = total
    gwo[col] = total
    for k in (2, 3, 1):
        send(remote(gwf, gwo.at[col], fs_sem.at[k - 1], fr_sem.at[col], row, col_at(k)))
    gr_sum = grs[row]
    for k in range(1, n):
        at = row_at(k)
        pltpu.make_async_copy(grs.at[at], grb.at[at], hr_sem.at[at]).wait()
        gr_sum += grb[at]
    for j in range(right_count):
        gr_ref[pl.ds(j, share, stride=right_count), :] = gr_sum[:, j * width:(j + 1) * width]
    pltpu.make_async_copy(gln, glf, g2r_sem).wait()
    gl_own = glf[...]
    for i in range(left_count):
        gl_ref[pl.ds(i, share, stride=left_count), :] = gl_own[:, i * width:(i + 1) * width]
    for k in range(1, n):
        at = col_at(k)
        pltpu.make_async_copy(gwf, gwo.at[at], fr_sem.at[at]).wait()
    for k in range(n):
        for d in range(slice_width):
            gw_ref[pl.ds(k * slice_width + d, width // n, stride=width), :] = gwo[k, d]

    for copy in sends:
        copy.wait_send()

    @pl.when(jnp.logical_not(diagonal))
    def _():
        l_out.wait_send()
        gl_out.wait_send()


def store_kernel(*refs):
    count = (len(refs) - 1) // 2
    sems = refs[-1]
    copies = [
        pltpu.make_async_copy(refs[k], refs[count + k], sems.at[k]) for k in range(count)
    ]
    for copy in copies:
        copy.start()
    for copy in copies:
        copy.wait()


def fused(n, left_act, right_act, weight, bias, cotangent):
    share, right_count, width = right_act.shape
    left_count = cotangent.shape[0]
    pair_width = weight.shape[1]
    seqs = share * n
    f32 = jnp.float32
    left_lanes, right_lanes = left_count * width, right_count * width
    pairs = left_count * right_count
    slice_width = width // n
    dma = pltpu.SemaphoreType.DMA
    anywhere = pl.BlockSpec(memory_space=pl.ANY)
    vmem = pl.BlockSpec(memory_space=pltpu.VMEM)
    shapes = (
        (pairs, pair_width),
        (share * left_count, width),
        (share * right_count, width),
        (width * width // n, pair_width),
    )
    held = pl.pallas_call(
        functools.partial(fused_kernel, n, seqs, left_count, right_count, width),
        out_shape=tuple(pltpu.VMEM(shape, f32) for shape in shapes),
        in_specs=[anywhere, anywhere, anywhere, vmem, anywhere],
        out_specs=(vmem,) * len(shapes),
        scratch_shapes=[
            pltpu.VMEM((share * left_count, width), f32),
            pltpu.VMEM((share * right_count, width), f32),
            pltpu.VMEM(weight.shape, f32),
            pltpu.VMEM((share, left_lanes), f32),
            pltpu.VMEM((share, right_lanes), f32),
            pltpu.VMEM((n, share, left_lanes), f32),
            pltpu.VMEM((n, share, right_lanes), f32),
            pltpu.VMEM((n, pairs, pair_width), f32),
            pltpu.VMEM((left_lanes, seqs), f32),
            pltpu.VMEM((right_lanes, seqs), f32),
            pltpu.VMEM((n, right_count * slice_width, seqs), f32),
            pltpu.VMEM((n, right_count * slice_width, seqs), f32),
            pltpu.VMEM((pairs, width * width), f32),
            pltpu.VMEM((left_count * right_count * n, slice_width * width), f32),
            pltpu.VMEM((left_lanes, right_lanes), f32),
            pltpu.VMEM((slice_width, n, width // n, pair_width), f32),
            pltpu.VMEM((n, slice_width, width // n, pair_width), f32),
            pltpu.VMEM((slice_width, width // n, pair_width), f32),
            pltpu.VMEM((n, slice_width, width // n, pair_width), f32),
            pltpu.VMEM((n, share, left_lanes), f32),
            pltpu.VMEM((n, share, left_lanes), f32),
            pltpu.VMEM((share, left_lanes), f32),
            pltpu.VMEM((share, left_lanes), f32),
            pltpu.VMEM((n, share, right_lanes), f32),
            pltpu.VMEM((n, share, right_lanes), f32),
            dma((4,)), dma((n - 1,)), dma((n,)), dma(()), dma((n,)), dma((n - 1,)),
            dma((n - 1,)), dma((n,)), dma((n - 1,)), dma((n,)),
            dma((n - 1,)), dma((n,)), dma((n - 1,)), dma((n,)),
            dma((n - 1,)), dma((n,)), dma(()), dma(()), dma((n - 1,)), dma((n,)),
        ],
        compiler_params=pltpu.CompilerParams(collective_id=0, has_side_effects=True),
    )(
        left_act.reshape(share * right_count, width),
        right_act.reshape(share * right_count, width),
        weight,
        bias.reshape(1, pair_width),
        cotangent.reshape(pairs, pair_width),
    )
    pair, gl, gr, gw = pl.pallas_call(
        store_kernel,
        out_shape=tuple(jax.ShapeDtypeStruct(shape, f32) for shape in shapes),
        in_specs=[vmem] * len(shapes),
        out_specs=(anywhere,) * len(shapes),
        scratch_shapes=[dma((len(shapes),))],
    )(*[pltpu.with_memory_space_constraint(x, pltpu.VMEM) for x in held])
    return (
        pair.reshape(cotangent.shape),
        gl.reshape(left_act.shape),
        gr.reshape(right_act.shape),
        gw,
    )


def block_terms(left_block, right_full, cot_block, weight_cube, bias):
    seqs = right_full.shape[0]
    highest = lax.Precision.HIGHEST
    products = jnp.einsum("sic,sjd->icjd", left_block, right_full, precision=highest) / seqs
    pair_block = jnp.einsum("icjd,cdz->ijz", products, weight_cube, precision=highest) + bias
    grad_outer = jnp.einsum("ijz,cdz->icjd", cot_block, weight_cube, precision=highest)
    weight_term = jnp.einsum("icjd,ijz->cdz", products, cot_block, precision=highest)
    left_term = jnp.einsum("icjd,sjd->sic", grad_outer, right_full, precision=highest) / seqs
    right_term = jnp.einsum("icjd,sic->sjd", grad_outer, left_block, precision=highest) / seqs
    return (pair_block, weight_term, left_term, right_term)


def general(left_act, right_act, weight, bias, cotangent):
    width = left_act.shape[2]
    pair_width = weight.shape[1]
    widened = lax.all_gather(left_act, "col", axis=1, tiled=True)
    left_full = lax.all_to_all(widened, "row", split_axis=1, concat_axis=0, tiled=True)
    right_full = lax.all_gather(right_act, "row", axis=0, tiled=True)
    weight_cube = weight.reshape(width, width, pair_width)
    pair, grad_cube, left_partial, right_partial = block_terms(
        left_full, right_full, cotangent, weight_cube, bias
    )
    returned = lax.all_to_all(left_partial, "row", split_axis=0, concat_axis=1, tiled=True)
    grad_left = lax.psum_scatter(returned, "col", scatter_dimension=1, tiled=True)
    grad_right = lax.psum_scatter(right_partial, "row", scatter_dimension=0, tiled=True)
    grad_flat = grad_cube.reshape(width * width, pair_width)
    weight_part = lax.psum_scatter(grad_flat, "row", scatter_dimension=0, tiled=True)
    grad_weight = lax.psum(weight_part, "col")
    return (pair, grad_left, grad_right, grad_weight)


def shards(rows, cols, left_act, right_act, weight, bias, cotangent):
    share, right_count, width = right_act.shape
    left_count = cotangent.shape[0]
    fits = (
        rows == cols == 4
        and left_count == right_count == SUBLANES
        and share % SUBLANES == 0
        and share * rows == LANES
        and 4 * width == LANES
        and weight.shape[1] == LANES
    )
    if fits:
        return fused(rows, left_act, right_act, weight, bias, cotangent)
    return general(left_act, right_act, weight, bias, cotangent)


def solution(mesh):
    placed = (
        P(("groups", "row"), "col", None),
        P(("groups", "row"), "col", None),
        P(),
        P(),
        P(("groups", "row"), "col", None),
    )
    return jax.shard_map(
        functools.partial(shards, mesh.shape["row"], mesh.shape["col"]),
        mesh=mesh,
        in_specs=placed,
        out_specs=(
            P(("groups", "row"), "col", None),
            P(("groups", "row"), "col", None),
            P(("groups", "row"), "col", None),
            P(("groups", "row"), None),
        ),
        check_vma=False,
    )
```

```python
import functools

import jax
import jax.numpy as jnp
from jax import lax
from jax.experimental import pallas as pl
from jax.experimental.pallas import tpu as pltpu
from jax.sharding import PartitionSpec as P

LANES = 128
SUBLANES = 8
NN = (((1,), (0,)), ((), ()))
NT = (((1,), (1,)), ((), ()))


def split(value):
    high = value.astype(jnp.bfloat16)
    low = (value - high.astype(jnp.float32)).astype(jnp.bfloat16)
    return high, low


def product(a, b, dims):
    dot = functools.partial(lax.dot_general, dimension_numbers=dims, preferred_element_type=jnp.float32)
    return dot(a[0], b[1]) + dot(a[1], b[0]) + dot(a[0], b[0])


def swap_groups(tiles, width):
    lane = lax.broadcasted_iota(jnp.int32, tiles[0].shape, 1)
    low_half = lane < 2 * width
    even = lax.rem(lane // width, 2) == 0
    x = list(tiles)
    for p in (0, 1):
        a, b = x[p], x[p + 2]
        x[p] = jnp.where(low_half, a, pltpu.roll(b, 2 * width, 1))
        x[p + 2] = jnp.where(low_half, pltpu.roll(a, 2 * width, 1), b)
    for p in (0, 2):
        a, b = x[p], x[p + 1]
        x[p] = jnp.where(even, a, pltpu.roll(b, width, 1))
        x[p + 1] = jnp.where(even, pltpu.roll(a, LANES - width, 1), b)
    return x


def fused_kernel(
    n, seqs, left_count, right_count, width,
    l_hbm, r_hbm, w_hbm, b_ref, c_hbm,
    pair_ref, gl_ref, gr_ref, gw_ref,
    l_in, r_in, wv, lpack, rpack, lbuf, rbuf, call, ltr, rtr, rsl, rq, o2, oq, gop,
    gws, gwz, gwf, gwo, gls, glc, gln, glf, grs, grb,
    in_sem, rs_sem, rr_sem, ls_sem, lr_sem, lf_sem, cs_sem, cr_sem, qs_sem, qr_sem,
    gs_sem, gr_sem, fs_sem, fr_sem, g1_sem, g1r_sem, g2_sem, g2r_sem, h_sem, hr_sem,
):
    group, row, col = lax.axis_index("groups"), lax.axis_index("row"), lax.axis_index("col")
    share = seqs // n
    quads = LANES // width
    halves = right_count // quads
    blocks = width // quads
    slice_width = width // n
    seq_scale = 1.0 / seqs

    def remote(src, dst, send, recv, to_row, to_col):
        return pltpu.make_async_remote_copy(
            src_ref=src, dst_ref=dst, send_sem=send, recv_sem=recv,
            device_id=(group, to_row, to_col), device_id_type=pl.DeviceIdType.MESH,
        )

    def peer(at, k):
        return (at + 1 - 2 * lax.rem(at, 2), lax.rem(at + n // 2, n), n - 1 - at)[k - 1]

    def row_at(k):
        return peer(row, k)

    def col_at(k):
        return peer(col, k)

    diagonal = row == col
    barrier = pltpu.get_barrier_semaphore()

    def greet(to_row, to_col):
        pl.semaphore_signal(
            barrier, inc=1, device_id=(group, to_row, to_col), device_id_type=pl.DeviceIdType.MESH
        )

    for k in (3, 2, 1):
        greet(row_at(k), col)
    for k in (2, 3, 1):
        greet(row, col_at(k))

    @pl.when(jnp.logical_not(diagonal))
    def _():
        greet(col, row)

    @pl.when(diagonal)
    def _():
        greet(row_at(2), col_at(2))

    fetches = [
        pltpu.make_async_copy(src, dst, in_sem.at[k])
        for k, (src, dst) in enumerate(
            ((l_hbm, l_in), (r_hbm, r_in), (c_hbm, call.at[col]), (w_hbm, wv))
        )
    ]
    for fetch in fetches:
        fetch.start()
    fetches[0].wait()
    for i in range(left_count):
        lpack[:, i * width:(i + 1) * width] = l_in[pl.ds(i, share, stride=left_count), :]
    fetches[1].wait()
    for j in range(right_count):
        rpack[:, j * width:(j + 1) * width] = r_in[pl.ds(j, share, stride=right_count), :]
    rbuf[row] = rpack[...]
    fetches[2].wait()
    pl.semaphore_wait(barrier, 2 * (n - 1) + 1)

    sends = []

    def send(copy):
        copy.start()
        sends.append(copy)

    l_out = remote(lpack, lbuf.at[row], ls_sem, lr_sem.at[row], col, row)

    @pl.when(diagonal)
    def _():
        pltpu.make_async_copy(lpack, lbuf.at[row], lr_sem.at[row]).start()

    @pl.when(jnp.logical_not(diagonal))
    def _():
        l_out.start()

    for k in (3, 2, 1):
        send(remote(rpack, rbuf.at[row], rs_sem.at[k - 1], rr_sem.at[row], row_at(k), col))
    for k in (2, 3, 1):
        send(remote(call.at[col], call.at[col], cs_sem.at[k - 1], cr_sem.at[col], row, col_at(k)))

    cot = jnp.concatenate(
        [call[col, pl.ds(j, left_count, stride=right_count), :] for j in range(right_count)], axis=0
    )
    fetches[3].wait()
    w_parts = split(wv[...])
    go2 = product(split(cot), w_parts, NT) * seq_scale
    for h in range(halves):
        for q in range(blocks):
            tiles = [
                go2[(h * quads + b) * left_count:(h * quads + b + 1) * left_count, q * LANES:(q + 1) * LANES]
                for b in range(quads)
            ]
            for a, tile in enumerate(swap_groups(tiles, width)):
                at = (q * quads + a) * left_count
                gop[at:at + left_count, h * LANES:(h + 1) * LANES] = tile
    go_parts = split(gop[...])

    pltpu.make_async_copy(lpack, lbuf.at[col], lr_sem.at[col]).wait()
    for k in (2, 3, 1):
        send(remote(lbuf.at[col], lbuf.at[col], lf_sem.at[k - 1], lr_sem.at[col], row, col_at(k)))
    for k in range(1, n):
        pltpu.make_async_copy(rpack, rbuf.at[row_at(k)], rr_sem.at[row_at(k)]).wait()
    right = rbuf[...].reshape(seqs, right_count * width)
    rtr[...] = right.T
    for d in range(width):
        at = d % slice_width * right_count
        rsl[d // slice_width, at:at + right_count, :] = rtr[pl.ds(d, right_count, stride=width), :]
    for k in (2, 3, 1):
        send(remote(rsl.at[col_at(k)], rq.at[col], qs_sem.at[k - 1], qr_sem.at[col], row, col_at(k)))
    rq[col] = rsl[col]

    right_parts = split(right)
    glt = product(go_parts, right_parts, NT)
    for c in range(width):
        ltr[pl.ds(c, left_count, stride=width), :] = glt[c * left_count:(c + 1) * left_count, :]
    gls[...] = ltr[...].T.reshape(gls.shape)
    for k in (2, 3, 1):
        send(remote(gls.at[col_at(k)], glc.at[col], g1_sem.at[k - 1], g1r_sem.at[col], row, col_at(k)))

    for k in range(1, n):
        pltpu.make_async_copy(lpack, lbuf.at[col_at(k)], lr_sem.at[col_at(k)]).wait()
    left = lbuf[...].reshape(seqs, left_count * width)
    left_parts = split(left)
    ltr[...] = left.T
    left_t = jnp.concatenate(
        [ltr[pl.ds(c, left_count, stride=width), :] for c in range(width)], axis=0
    )
    grs[...] = product(split(left_t.T), go_parts, NN).reshape(grs.shape)
    for k in range(1, n):
        pltpu.make_async_copy(call.at[col], call.at[col_at(k)], cr_sem.at[col_at(k)]).wait()
    cot_all = jnp.concatenate(
        [
            call[k, i * right_count:(i + 1) * right_count, :]
            for i in range(left_count)
            for k in range(n)
        ],
        axis=0,
    )
    cot_t = split(cot_all.T)
    for k in range(1, n):
        pltpu.make_async_copy(rsl.at[col], rq.at[col_at(k)], qr_sem.at[col_at(k)]).wait()
    slice_t = jnp.concatenate(
        [
            rq[k, d * right_count:(d + 1) * right_count, :]
            for d in range(slice_width)
            for k in range(n)
        ],
        axis=0,
    )
    outer_q = product(split(slice_t), left_parts, NN) * seq_scale
    span = n * right_count
    for h in range(left_count // quads):
        for q in range(slice_width // quads):
            tiles = [
                outer_q[(q * quads + a) * span:(q * quads + a + 1) * span, h * LANES:(h + 1) * LANES]
                for a in range(quads)
            ]
            for b, tile in enumerate(swap_groups(tiles, width)):
                at = (h * quads + b) * span
                oq[at:at + span, q * LANES:(q + 1) * LANES] = tile
    gws[...] = product(cot_t, split(oq[...]), NN).T.reshape(gws.shape)
    for k in (3, 2, 1):
        send(remote(gws.at[:, row_at(k)], gwz.at[row], gs_sem.at[k - 1], gr_sem.at[row], row_at(k), col))

    for k in (3, 2, 1):
        send(remote(grs.at[row_at(k)], grb.at[row], h_sem.at[k - 1], hr_sem.at[row], row_at(k), col))

    for k in range(1, n):
        pltpu.make_async_copy(gls.at[col], glc.at[col_at(k)], g1r_sem.at[col_at(k)]).wait()
    gl_sum = gls[col]
    for k in range(1, n):
        gl_sum += glc[col_at(k)]
    gln[...] = gl_sum
    gl_out = remote(gln, glf, g2_sem, g2r_sem, col, row)

    @pl.when(diagonal)
    def _():
        pltpu.make_async_copy(gln, glf, g2r_sem).start()

    @pl.when(jnp.logical_not(diagonal))
    def _():
        gl_out.start()

    outer = product(split(left_t), right_parts, NN) * seq_scale
    for h in range(halves):
        for q in range(blocks):
            tiles = [
                outer[(q * quads + a) * left_count:(q * quads + a + 1) * left_count, h * LANES:(h + 1) * LANES]
                for a in range(quads)
            ]
            for b, tile in enumerate(swap_groups(tiles, width)):
                at = (h * quads + b) * left_count
                o2[at:at + left_count, q * LANES:(q + 1) * LANES] = tile
    pair = product(split(o2[...]), w_parts, NN) + b_ref[...]
    for j in range(right_count):
        pair_ref[pl.ds(j, left_count, stride=right_count), :] = pair[j * left_count:(j + 1) * left_count, :]

    total = gws[:, row]
    for k in range(1, n):
        at = row_at(k)
        pltpu.make_async_copy(gws.at[:, at], gwz.at[at], gr_sem.at[at]).wait()
        total += gwz[at]
    gwf[...] = total
    gwo[col] = total
    for k in (2, 3, 1):
        send(remote(gwf, gwo.at[col], fs_sem.at[k - 1], fr_sem.at[col], row, col_at(k)))
    gr_sum = grs[row]
    for k in range(1, n):
        at = row_at(k)
        pltpu.make_async_copy(grs.at[at], grb.at[at], hr_sem.at[at]).wait()
        gr_sum += grb[at]
    for j in range(right_count):
        gr_ref[pl.ds(j, share, stride=right_count), :] = gr_sum[:, j * width:(j + 1) * width]
    pltpu.make_async_copy(gln, glf, g2r_sem).wait()
    gl_own = glf[...]
    for i in range(left_count):
        gl_ref[pl.ds(i, share, stride=left_count), :] = gl_own[:, i * width:(i + 1) * width]
    for k in range(1, n):
        at = col_at(k)
        pltpu.make_async_copy(gwf, gwo.at[at], fr_sem.at[at]).wait()
    for k in range(n):
        for d in range(slice_width):
            gw_ref[pl.ds(k * slice_width + d, width // n, stride=width), :] = gwo[k, d]

    for copy in sends:
        copy.wait_send()

    @pl.when(jnp.logical_not(diagonal))
    def _():
        l_out.wait_send()
        gl_out.wait_send()


def store_kernel(*refs):
    count = (len(refs) - 1) // 2
    sems = refs[-1]
    copies = [
        pltpu.make_async_copy(refs[k], refs[count + k], sems.at[k]) for k in range(count)
    ]
    for copy in copies:
        copy.start()
    for copy in copies:
        copy.wait()


def fused(n, left_act, right_act, weight, bias, cotangent):
    share, right_count, width = right_act.shape
    left_count = cotangent.shape[0]
    pair_width = weight.shape[1]
    seqs = share * n
    f32 = jnp.float32
    left_lanes, right_lanes = left_count * width, right_count * width
    pairs = left_count * right_count
    slice_width = width // n
    dma = pltpu.SemaphoreType.DMA
    anywhere = pl.BlockSpec(memory_space=pl.ANY)
    vmem = pl.BlockSpec(memory_space=pltpu.VMEM)
    shapes = (
        (pairs, pair_width),
        (share * left_count, width),
        (share * right_count, width),
        (width * width // n, pair_width),
    )
    held = pl.pallas_call(
        functools.partial(fused_kernel, n, seqs, left_count, right_count, width),
        out_shape=tuple(pltpu.VMEM(shape, f32) for shape in shapes),
        in_specs=[anywhere, anywhere, anywhere, vmem, anywhere],
        out_specs=(vmem,) * len(shapes),
        scratch_shapes=[
            pltpu.VMEM((share * left_count, width), f32),
            pltpu.VMEM((share * right_count, width), f32),
            pltpu.VMEM(weight.shape, f32),
            pltpu.VMEM((share, left_lanes), f32),
            pltpu.VMEM((share, right_lanes), f32),
            pltpu.VMEM((n, share, left_lanes), f32),
            pltpu.VMEM((n, share, right_lanes), f32),
            pltpu.VMEM((n, pairs, pair_width), f32),
            pltpu.VMEM((left_lanes, seqs), f32),
            pltpu.VMEM((right_lanes, seqs), f32),
            pltpu.VMEM((n, right_count * slice_width, seqs), f32),
            pltpu.VMEM((n, right_count * slice_width, seqs), f32),
            pltpu.VMEM((pairs, width * width), f32),
            pltpu.VMEM((left_count * right_count * n, slice_width * width), f32),
            pltpu.VMEM((left_lanes, right_lanes), f32),
            pltpu.VMEM((slice_width, n, width // n, pair_width), f32),
            pltpu.VMEM((n, slice_width, width // n, pair_width), f32),
            pltpu.VMEM((slice_width, width // n, pair_width), f32),
            pltpu.VMEM((n, slice_width, width // n, pair_width), f32),
            pltpu.VMEM((n, share, left_lanes), f32),
            pltpu.VMEM((n, share, left_lanes), f32),
            pltpu.VMEM((share, left_lanes), f32),
            pltpu.VMEM((share, left_lanes), f32),
            pltpu.VMEM((n, share, right_lanes), f32),
            pltpu.VMEM((n, share, right_lanes), f32),
            dma((4,)), dma((n - 1,)), dma((n,)), dma(()), dma((n,)), dma((n - 1,)),
            dma((n - 1,)), dma((n,)), dma((n - 1,)), dma((n,)),
            dma((n - 1,)), dma((n,)), dma((n - 1,)), dma((n,)),
            dma((n - 1,)), dma((n,)), dma(()), dma(()), dma((n - 1,)), dma((n,)),
        ],
        compiler_params=pltpu.CompilerParams(collective_id=0, has_side_effects=True),
    )(
        left_act.reshape(share * right_count, width),
        right_act.reshape(share * right_count, width),
        weight,
        bias.reshape(1, pair_width),
        cotangent.reshape(pairs, pair_width),
    )
    pair, gl, gr, gw = pl.pallas_call(
        store_kernel,
        out_shape=tuple(jax.ShapeDtypeStruct(shape, f32) for shape in shapes),
        in_specs=[vmem] * len(shapes),
        out_specs=(anywhere,) * len(shapes),
        scratch_shapes=[dma((len(shapes),))],
    )(*[pltpu.with_memory_space_constraint(x, pltpu.VMEM) for x in held])
    return (
        pair.reshape(cotangent.shape),
        gl.reshape(left_act.shape),
        gr.reshape(right_act.shape),
        gw,
    )


def block_terms(left_block, right_full, cot_block, weight_cube, bias):
    seqs = right_full.shape[0]
    highest = lax.Precision.HIGHEST
    products = jnp.einsum("sic,sjd->icjd", left_block, right_full, precision=highest) / seqs
    pair_block = jnp.einsum("icjd,cdz->ijz", products, weight_cube, precision=highest) + bias
    grad_outer = jnp.einsum("ijz,cdz->icjd", cot_block, weight_cube, precision=highest)
    weight_term = jnp.einsum("icjd,ijz->cdz", products, cot_block, precision=highest)
    left_term = jnp.einsum("icjd,sjd->sic", grad_outer, right_full, precision=highest) / seqs
    right_term = jnp.einsum("icjd,sic->sjd", grad_outer, left_block, precision=highest) / seqs
    return (pair_block, weight_term, left_term, right_term)


def general(left_act, right_act, weight, bias, cotangent):
    width = left_act.shape[2]
    pair_width = weight.shape[1]
    widened = lax.all_gather(left_act, "col", axis=1, tiled=True)
    left_full = lax.all_to_all(widened, "row", split_axis=1, concat_axis=0, tiled=True)
    right_full = lax.all_gather(right_act, "row", axis=0, tiled=True)
    weight_cube = weight.reshape(width, width, pair_width)
    pair, grad_cube, left_partial, right_partial = block_terms(
        left_full, right_full, cotangent, weight_cube, bias
    )
    returned = lax.all_to_all(left_partial, "row", split_axis=0, concat_axis=1, tiled=True)
    grad_left = lax.psum_scatter(returned, "col", scatter_dimension=1, tiled=True)
    grad_right = lax.psum_scatter(right_partial, "row", scatter_dimension=0, tiled=True)
    grad_flat = grad_cube.reshape(width * width, pair_width)
    weight_part = lax.psum_scatter(grad_flat, "row", scatter_dimension=0, tiled=True)
    grad_weight = lax.psum(weight_part, "col")
    return (pair, grad_left, grad_right, grad_weight)


def shards(rows, cols, left_act, right_act, weight, bias, cotangent):
    share, right_count, width = right_act.shape
    left_count = cotangent.shape[0]
    fits = (
        rows == cols == 4
        and left_count == right_count == SUBLANES
        and share % SUBLANES == 0
        and share * rows == LANES
        and 4 * width == LANES
        and weight.shape[1] == LANES
    )
    if fits:
        return fused(rows, left_act, right_act, weight, bias, cotangent)
    return general(left_act, right_act, weight, bias, cotangent)


def solution(mesh):
    placed = (
        P(("groups", "row"), "col", None),
        P(("groups", "row"), "col", None),
        P(),
        P(),
        P(("groups", "row"), "col", None),
    )
    return jax.shard_map(
        functools.partial(shards, mesh.shape["row"], mesh.shape["col"]),
        mesh=mesh,
        in_specs=placed,
        out_specs=(
            P(("groups", "row"), "col", None),
            P(("groups", "row"), "col", None),
            P(("groups", "row"), "col", None),
            P(("groups", "row"), None),
        ),
        check_vma=False,
    )
```

```python
import functools

import jax
import jax.numpy as jnp
from jax import lax
from jax.experimental import pallas as pl
from jax.experimental.pallas import tpu as pltpu
from jax.sharding import PartitionSpec as P

LANES = 128
SUBLANES = 8
NN = (((1,), (0,)), ((), ()))
NT = (((1,), (1,)), ((), ()))


def split(value):
    high = value.astype(jnp.bfloat16)
    low = (value - high.astype(jnp.float32)).astype(jnp.bfloat16)
    return high, low


def product(a, b, dims):
    dot = functools.partial(lax.dot_general, dimension_numbers=dims, preferred_element_type=jnp.float32)
    return dot(a[0], b[1]) + dot(a[1], b[0]) + dot(a[0], b[0])


def swap_groups(tiles, width):
    lane = lax.broadcasted_iota(jnp.int32, tiles[0].shape, 1)
    low_half = lane < 2 * width
    even = lax.rem(lane // width, 2) == 0
    x = list(tiles)
    for p in (0, 1):
        a, b = x[p], x[p + 2]
        x[p] = jnp.where(low_half, a, pltpu.roll(b, 2 * width, 1))
        x[p + 2] = jnp.where(low_half, pltpu.roll(a, 2 * width, 1), b)
    for p in (0, 2):
        a, b = x[p], x[p + 1]
        x[p] = jnp.where(even, a, pltpu.roll(b, width, 1))
        x[p + 1] = jnp.where(even, pltpu.roll(a, LANES - width, 1), b)
    return x


def fused_kernel(
    n, seqs, left_count, right_count, width,
    l_hbm, r_hbm, w_hbm, b_ref, c_hbm,
    pair_ref, gl_ref, gr_ref, gw_ref,
    l_in, r_in, wv, lpack, rpack, lbuf, rbuf, call, ltr, rtr, rsl, rq, o2, oq, gop,
    gws, gwz, gwf, gwo, gls, glc, gln, glf, grs, grb,
    in_sem, rs_sem, rr_sem, ls_sem, lr_sem, lf_sem, cs_sem, cr_sem, qs_sem, qr_sem,
    gs_sem, gr_sem, fs_sem, fr_sem, g1_sem, g1r_sem, g2_sem, g2r_sem, h_sem, hr_sem,
):
    group, row, col = lax.axis_index("groups"), lax.axis_index("row"), lax.axis_index("col")
    share = seqs // n
    quads = LANES // width
    halves = right_count // quads
    blocks = width // quads
    slice_width = width // n
    seq_scale = 1.0 / seqs

    def remote(src, dst, send, recv, to_row, to_col):
        return pltpu.make_async_remote_copy(
            src_ref=src, dst_ref=dst, send_sem=send, recv_sem=recv,
            device_id=(group, to_row, to_col), device_id_type=pl.DeviceIdType.MESH,
        )

    def peer(at, k):
        return (at + 1 - 2 * lax.rem(at, 2), lax.rem(at + n // 2, n), n - 1 - at)[k - 1]

    def row_at(k):
        return peer(row, k)

    def col_at(k):
        return peer(col, k)

    diagonal = row == col
    barrier = pltpu.get_barrier_semaphore()

    def greet(to_row, to_col):
        pl.semaphore_signal(
            barrier, inc=1, device_id=(group, to_row, to_col), device_id_type=pl.DeviceIdType.MESH
        )

    for k in (3, 2, 1):
        greet(row_at(k), col)
    for k in (2, 3, 1):
        greet(row, col_at(k))

    @pl.when(jnp.logical_not(diagonal))
    def _():
        greet(col, row)

    @pl.when(diagonal)
    def _():
        greet(row_at(2), col_at(2))

    fetches = [
        pltpu.make_async_copy(src, dst, in_sem.at[k])
        for k, (src, dst) in enumerate(
            ((l_hbm, l_in), (r_hbm, r_in), (c_hbm, call.at[col]), (w_hbm, wv))
        )
    ]
    for fetch in fetches:
        fetch.start()
    fetches[0].wait()
    for i in range(left_count):
        lpack[:, i * width:(i + 1) * width] = l_in[pl.ds(i, share, stride=left_count), :]
    fetches[1].wait()
    for j in range(right_count):
        rpack[:, j * width:(j + 1) * width] = r_in[pl.ds(j, share, stride=right_count), :]
    rbuf[row] = rpack[...]
    fetches[2].wait()
    pl.semaphore_wait(barrier, 2 * (n - 1) + 1)

    sends = []

    def send(copy):
        copy.start()
        sends.append(copy)

    l_out = remote(lpack, lbuf.at[row], ls_sem, lr_sem.at[row], col, row)

    @pl.when(diagonal)
    def _():
        pltpu.make_async_copy(lpack, lbuf.at[row], lr_sem.at[row]).start()

    @pl.when(jnp.logical_not(diagonal))
    def _():
        l_out.start()

    for k in (3, 2, 1):
        send(remote(rpack, rbuf.at[row], rs_sem.at[k - 1], rr_sem.at[row], row_at(k), col))
    for k in (2, 3, 1):
        send(remote(call.at[col], call.at[col], cs_sem.at[k - 1], cr_sem.at[col], row, col_at(k)))

    cot = jnp.concatenate(
        [call[col, pl.ds(j, left_count, stride=right_count), :] for j in range(right_count)], axis=0
    )
    fetches[3].wait()
    w_parts = split(wv[...])
    go2 = product(split(cot), w_parts, NT) * seq_scale
    for h in range(halves):
        for q in range(blocks):
            tiles = [
                go2[(h * quads + b) * left_count:(h * quads + b + 1) * left_count, q * LANES:(q + 1) * LANES]
                for b in range(quads)
            ]
            for a, tile in enumerate(swap_groups(tiles, width)):
                at = (q * quads + a) * left_count
                gop[at:at + left_count, h * LANES:(h + 1) * LANES] = tile
    go_parts = split(gop[...])

    pltpu.make_async_copy(lpack, lbuf.at[col], lr_sem.at[col]).wait()
    for k in (2, 3, 1):
        send(remote(lbuf.at[col], lbuf.at[col], lf_sem.at[k - 1], lr_sem.at[col], row, col_at(k)))
    for k in range(1, n):
        pltpu.make_async_copy(rpack, rbuf.at[row_at(k)], rr_sem.at[row_at(k)]).wait()
    right = rbuf[...].reshape(seqs, right_count * width)
    rtr[...] = right.T
    for d in range(width):
        at = d % slice_width * right_count
        rsl[d // slice_width, at:at + right_count, :] = rtr[pl.ds(d, right_count, stride=width), :]
    for k in (2, 3, 1):
        send(remote(rsl.at[col_at(k)], rq.at[col], qs_sem.at[k - 1], qr_sem.at[col], row, col_at(k)))
    rq[col] = rsl[col]

    right_parts = split(right)
    glt = product(go_parts, right_parts, NT)
    for c in range(width):
        ltr[pl.ds(c, left_count, stride=width), :] = glt[c * left_count:(c + 1) * left_count, :]
    gls[...] = ltr[...].T.reshape(gls.shape)
    for k in (2, 3, 1):
        send(remote(gls.at[col_at(k)], glc.at[col], g1_sem.at[k - 1], g1r_sem.at[col], row, col_at(k)))

    for k in range(1, n):
        pltpu.make_async_copy(lpack, lbuf.at[col_at(k)], lr_sem.at[col_at(k)]).wait()
    left = lbuf[...].reshape(seqs, left_count * width)
    left_parts = split(left)
    ltr[...] = left.T
    left_t = jnp.concatenate(
        [ltr[pl.ds(c, left_count, stride=width), :] for c in range(width)], axis=0
    )
    grs[...] = product(split(left_t.T), go_parts, NN).reshape(grs.shape)
    for k in range(1, n):
        pltpu.make_async_copy(call.at[col], call.at[col_at(k)], cr_sem.at[col_at(k)]).wait()
    cot_all = jnp.concatenate(
        [
            call[k, i * right_count:(i + 1) * right_count, :]
            for i in range(left_count)
            for k in range(n)
        ],
        axis=0,
    )
    cot_t = split(cot_all.T)
    for k in range(1, n):
        pltpu.make_async_copy(rsl.at[col], rq.at[col_at(k)], qr_sem.at[col_at(k)]).wait()
    slice_t = jnp.concatenate(
        [
            rq[k, d * right_count:(d + 1) * right_count, :]
            for d in range(slice_width)
            for k in range(n)
        ],
        axis=0,
    )
    outer_q = product(split(slice_t), left_parts, NN) * seq_scale
    span = n * right_count
    for h in range(left_count // quads):
        for q in range(slice_width // quads):
            tiles = [
                outer_q[(q * quads + a) * span:(q * quads + a + 1) * span, h * LANES:(h + 1) * LANES]
                for a in range(quads)
            ]
            for b, tile in enumerate(swap_groups(tiles, width)):
                at = (h * quads + b) * span
                oq[at:at + span, q * LANES:(q + 1) * LANES] = tile
    gws[...] = product(cot_t, split(oq[...]), NN).T.reshape(gws.shape)
    for k in (3, 2, 1):
        send(remote(gws.at[:, row_at(k)], gwz.at[row], gs_sem.at[k - 1], gr_sem.at[row], row_at(k), col))

    for k in (1, 2, 3):
        send(remote(grs.at[row_at(k)], grb.at[row], h_sem.at[k - 1], hr_sem.at[row], row_at(k), col))

    for k in range(1, n):
        pltpu.make_async_copy(gls.at[col], glc.at[col_at(k)], g1r_sem.at[col_at(k)]).wait()
    gl_sum = gls[col]
    for k in range(1, n):
        gl_sum += glc[col_at(k)]
    gln[...] = gl_sum
    gl_out = remote(gln, glf, g2_sem, g2r_sem, col, row)

    @pl.when(diagonal)
    def _():
        pltpu.make_async_copy(gln, glf, g2r_sem).start()

    @pl.when(jnp.logical_not(diagonal))
    def _():
        gl_out.start()

    outer = product(split(left_t), right_parts, NN) * seq_scale
    for h in range(halves):
        for q in range(blocks):
            tiles = [
                outer[(q * quads + a) * left_count:(q * quads + a + 1) * left_count, h * LANES:(h + 1) * LANES]
                for a in range(quads)
            ]
            for b, tile in enumerate(swap_groups(tiles, width)):
                at = (h * quads + b) * left_count
                o2[at:at + left_count, q * LANES:(q + 1) * LANES] = tile
    pair = product(split(o2[...]), w_parts, NN) + b_ref[...]
    for j in range(right_count):
        pair_ref[pl.ds(j, left_count, stride=right_count), :] = pair[j * left_count:(j + 1) * left_count, :]

    total = gws[:, row]
    for k in range(1, n):
        at = row_at(k)
        pltpu.make_async_copy(gws.at[:, at], gwz.at[at], gr_sem.at[at]).wait()
        total += gwz[at]
    gwf[...] = total
    gwo[col] = total
    for k in (2, 3, 1):
        send(remote(gwf, gwo.at[col], fs_sem.at[k - 1], fr_sem.at[col], row, col_at(k)))
    gr_sum = grs[row]
    for k in range(1, n):
        at = row_at(k)
        pltpu.make_async_copy(grs.at[at], grb.at[at], hr_sem.at[at]).wait()
        gr_sum += grb[at]
    for j in range(right_count):
        gr_ref[pl.ds(j, share, stride=right_count), :] = gr_sum[:, j * width:(j + 1) * width]
    pltpu.make_async_copy(gln, glf, g2r_sem).wait()
    gl_own = glf[...]
    for i in range(left_count):
        gl_ref[pl.ds(i, share, stride=left_count), :] = gl_own[:, i * width:(i + 1) * width]
    for k in range(1, n):
        at = col_at(k)
        pltpu.make_async_copy(gwf, gwo.at[at], fr_sem.at[at]).wait()
    for k in range(n):
        for d in range(slice_width):
            gw_ref[pl.ds(k * slice_width + d, width // n, stride=width), :] = gwo[k, d]

    for copy in sends:
        copy.wait_send()

    @pl.when(jnp.logical_not(diagonal))
    def _():
        l_out.wait_send()
        gl_out.wait_send()


def store_kernel(*refs):
    count = (len(refs) - 1) // 2
    sems = refs[-1]
    copies = [
        pltpu.make_async_copy(refs[k], refs[count + k], sems.at[k]) for k in range(count)
    ]
    for copy in copies:
        copy.start()
    for copy in copies:
        copy.wait()


def fused(n, left_act, right_act, weight, bias, cotangent):
    share, right_count, width = right_act.shape
    left_count = cotangent.shape[0]
    pair_width = weight.shape[1]
    seqs = share * n
    f32 = jnp.float32
    left_lanes, right_lanes = left_count * width, right_count * width
    pairs = left_count * right_count
    slice_width = width // n
    dma = pltpu.SemaphoreType.DMA
    anywhere = pl.BlockSpec(memory_space=pl.ANY)
    vmem = pl.BlockSpec(memory_space=pltpu.VMEM)
    shapes = (
        (pairs, pair_width),
        (share * left_count, width),
        (share * right_count, width),
        (width * width // n, pair_width),
    )
    held = pl.pallas_call(
        functools.partial(fused_kernel, n, seqs, left_count, right_count, width),
        out_shape=tuple(pltpu.VMEM(shape, f32) for shape in shapes),
        in_specs=[anywhere, anywhere, anywhere, vmem, anywhere],
        out_specs=(vmem,) * len(shapes),
        scratch_shapes=[
            pltpu.VMEM((share * left_count, width), f32),
            pltpu.VMEM((share * right_count, width), f32),
            pltpu.VMEM(weight.shape, f32),
            pltpu.VMEM((share, left_lanes), f32),
            pltpu.VMEM((share, right_lanes), f32),
            pltpu.VMEM((n, share, left_lanes), f32),
            pltpu.VMEM((n, share, right_lanes), f32),
            pltpu.VMEM((n, pairs, pair_width), f32),
            pltpu.VMEM((left_lanes, seqs), f32),
            pltpu.VMEM((right_lanes, seqs), f32),
            pltpu.VMEM((n, right_count * slice_width, seqs), f32),
            pltpu.VMEM((n, right_count * slice_width, seqs), f32),
            pltpu.VMEM((pairs, width * width), f32),
            pltpu.VMEM((left_count * right_count * n, slice_width * width), f32),
            pltpu.VMEM((left_lanes, right_lanes), f32),
            pltpu.VMEM((slice_width, n, width // n, pair_width), f32),
            pltpu.VMEM((n, slice_width, width // n, pair_width), f32),
            pltpu.VMEM((slice_width, width // n, pair_width), f32),
            pltpu.VMEM((n, slice_width, width // n, pair_width), f32),
            pltpu.VMEM((n, share, left_lanes), f32),
            pltpu.VMEM((n, share, left_lanes), f32),
            pltpu.VMEM((share, left_lanes), f32),
            pltpu.VMEM((share, left_lanes), f32),
            pltpu.VMEM((n, share, right_lanes), f32),
            pltpu.VMEM((n, share, right_lanes), f32),
            dma((4,)), dma((n - 1,)), dma((n,)), dma(()), dma((n,)), dma((n - 1,)),
            dma((n - 1,)), dma((n,)), dma((n - 1,)), dma((n,)),
            dma((n - 1,)), dma((n,)), dma((n - 1,)), dma((n,)),
            dma((n - 1,)), dma((n,)), dma(()), dma(()), dma((n - 1,)), dma((n,)),
        ],
        compiler_params=pltpu.CompilerParams(collective_id=0, has_side_effects=True),
    )(
        left_act.reshape(share * right_count, width),
        right_act.reshape(share * right_count, width),
        weight,
        bias.reshape(1, pair_width),
        cotangent.reshape(pairs, pair_width),
    )
    pair, gl, gr, gw = pl.pallas_call(
        store_kernel,
        out_shape=tuple(jax.ShapeDtypeStruct(shape, f32) for shape in shapes),
        in_specs=[vmem] * len(shapes),
        out_specs=(anywhere,) * len(shapes),
        scratch_shapes=[dma((len(shapes),))],
    )(*[pltpu.with_memory_space_constraint(x, pltpu.VMEM) for x in held])
    return (
        pair.reshape(cotangent.shape),
        gl.reshape(left_act.shape),
        gr.reshape(right_act.shape),
        gw,
    )


def block_terms(left_block, right_full, cot_block, weight_cube, bias):
    seqs = right_full.shape[0]
    highest = lax.Precision.HIGHEST
    products = jnp.einsum("sic,sjd->icjd", left_block, right_full, precision=highest) / seqs
    pair_block = jnp.einsum("icjd,cdz->ijz", products, weight_cube, precision=highest) + bias
    grad_outer = jnp.einsum("ijz,cdz->icjd", cot_block, weight_cube, precision=highest)
    weight_term = jnp.einsum("icjd,ijz->cdz", products, cot_block, precision=highest)
    left_term = jnp.einsum("icjd,sjd->sic", grad_outer, right_full, precision=highest) / seqs
    right_term = jnp.einsum("icjd,sic->sjd", grad_outer, left_block, precision=highest) / seqs
    return (pair_block, weight_term, left_term, right_term)


def general(left_act, right_act, weight, bias, cotangent):
    width = left_act.shape[2]
    pair_width = weight.shape[1]
    widened = lax.all_gather(left_act, "col", axis=1, tiled=True)
    left_full = lax.all_to_all(widened, "row", split_axis=1, concat_axis=0, tiled=True)
    right_full = lax.all_gather(right_act, "row", axis=0, tiled=True)
    weight_cube = weight.reshape(width, width, pair_width)
    pair, grad_cube, left_partial, right_partial = block_terms(
        left_full, right_full, cotangent, weight_cube, bias
    )
    returned = lax.all_to_all(left_partial, "row", split_axis=0, concat_axis=1, tiled=True)
    grad_left = lax.psum_scatter(returned, "col", scatter_dimension=1, tiled=True)
    grad_right = lax.psum_scatter(right_partial, "row", scatter_dimension=0, tiled=True)
    grad_flat = grad_cube.reshape(width * width, pair_width)
    weight_part = lax.psum_scatter(grad_flat, "row", scatter_dimension=0, tiled=True)
    grad_weight = lax.psum(weight_part, "col")
    return (pair, grad_left, grad_right, grad_weight)


def shards(rows, cols, left_act, right_act, weight, bias, cotangent):
    share, right_count, width = right_act.shape
    left_count = cotangent.shape[0]
    fits = (
        rows == cols == 4
        and left_count == right_count == SUBLANES
        and share % SUBLANES == 0
        and share * rows == LANES
        and 4 * width == LANES
        and weight.shape[1] == LANES
    )
    if fits:
        return fused(rows, left_act, right_act, weight, bias, cotangent)
    return general(left_act, right_act, weight, bias, cotangent)


def solution(mesh):
    placed = (
        P(("groups", "row"), "col", None),
        P(("groups", "row"), "col", None),
        P(),
        P(),
        P(("groups", "row"), "col", None),
    )
    return jax.shard_map(
        functools.partial(shards, mesh.shape["row"], mesh.shape["col"]),
        mesh=mesh,
        in_specs=placed,
        out_specs=(
            P(("groups", "row"), "col", None),
            P(("groups", "row"), "col", None),
            P(("groups", "row"), "col", None),
            P(("groups", "row"), None),
        ),
        check_vma=False,
    )
```
